256 devices in a mesh: tm: 64 (over x, y, z_lo), space: 4 (over z_hi, core).
Axes of the slice: x: 4, y: 4, z: 8 (z_hi: 2, z_lo: 4; z = z_hi * 4 + z_lo), core: 2. Of those that a mesh axis runs over, the one named last changes fastest.
Arguments:
- latents: bfloat16 [1, 128, 16, 32, 256], P(None, 'tm', 'space'), may hold values from -24 to 24
- gain_one: float32 [256], replicated, may hold values from 0.25 to 1.75
- conv_one: bfloat16 [3, 3, 3, 256, 256], replicated, may hold values from -0.078125 to 0.078125
- gain_two: float32 [256], replicated, may hold values from 0.25 to 1.75
- conv_two: bfloat16 [3, 3, 3, 256, 256], replicated, may hold values from -0.078125 to 0.078125
- upsample: bfloat16 [3, 256, 256], replicated, may hold values from -0.375 to 0.375
Outputs:
- frames_out: bfloat16 [1, 256, 16, 32, 256], P(None, 'tm', 'space')
The draws below stay inside these ranges and needn't reach their ends.
All inputs are finite; a program needn't handle non-finite values.
Results may differ from the reference program's by a relative error of at most 0.008.
Values may be sent and summed in bfloat16 or wider, within the bound.
No kernel may reach another device: no remote copies, remote signals or barrier semaphores. Data moves between devices by JAX's collectives and lax.ppermute only.
A program may use at most 64 MiB of HBM per device.

```python
import math
import jax
import jax.numpy as jnp
from jax import lax

C = 256
V = 1
W = 32
FRAMES = 128
HEIGHT = 16


def draw_latents(key, part):
    key_base, key_cell, key_channel = jax.random.split(key, 3)
    dims_all = (V, FRAMES, HEIGHT, W, C)
    cell_dims = (V, FRAMES, HEIGHT, W, 1)
    base = jnp.clip(jax.random.normal(key_base, dims_all, jnp.float32), -4.0, 4.0)
    cell_scale = jnp.exp(jax.random.uniform(key_cell, cell_dims, jnp.float32, math.log(0.3), math.log(3.0)))
    channel_scale = jnp.exp(jax.random.uniform(key_channel, (C,), jnp.float32, math.log(0.5), math.log(2.0)))
    values = base * cell_scale * channel_scale
    return jnp.clip(values, -24.0, 24.0).astype(jnp.bfloat16)


def bell_draw(own_key, extent, scale, limit, kind=jnp.bfloat16):
    drawn = scale * jax.random.normal(own_key, extent, jnp.float32)
    return jnp.clip(drawn, min=-limit, max=limit).astype(kind)


def setup_inputs(seed: int = 0) -> dict:
    streams_of = jax.random.split(jax.random.key(seed), 7)
    latents = draw_latents(jax.random.fold_in(streams_of[6], 71), 0)
    gain_one = jnp.clip(1.0 + 0.15 * jax.random.normal(streams_of[1], (C,), jnp.float32), 0.25, 1.75)
    conv_one = bell_draw(streams_of[2], (3, 3, 3, C, C), (27 * C) ** -0.5, 0.078125)
    gain_two = jnp.clip(1.0 + 0.15 * jax.random.normal(streams_of[3], (C,), jnp.float32), 0.25, 1.75)
    conv_two = bell_draw(streams_of[4], (3, 3, 3, C, C), (27 * C) ** -0.5, 0.078125)
    upsample = bell_draw(streams_of[5], (3, C, C), C ** -0.5, 0.375)
    return dict(latents=latents, gain_one=gain_one, conv_one=conv_one, gain_two=gain_two, conv_two=conv_two, upsample=upsample)


def normed_silu(features, gain_vec):
    values = features.astype(jnp.float32)
    mean_square = lax.optimization_barrier(jnp.mean(values * values, axis=-1, keepdims=True))
    return jax.nn.silu(values * lax.rsqrt(mean_square + 1e-06) * gain_vec.astype(jnp.float32)).astype(jnp.bfloat16)

def causal_conv(activation, weight):
    padded = jnp.pad(activation.astype(jnp.float32), ((0, 0), (2, 0), (1, 1), (1, 1), (0, 0)))
    return lax.conv_general_dilated(padded, weight.astype(jnp.float32), (1, 1, 1), 'VALID', dimension_numbers=('NDHWC', 'DHWIO', 'NDHWC'), precision=lax.Precision.HIGHEST)

def reference(latents, gain_one, conv_one, gain_two, conv_two, upsample):
    maps = upsample.astype(jnp.float32)

    def decode_video(features):
        first_input = normed_silu(features, gain_one)
        hidden = causal_conv(first_input[None], conv_one)[0].astype(jnp.bfloat16)
        second_input = normed_silu(hidden, gain_two)
        block_out = (features.astype(jnp.float32) + causal_conv(second_input[None], conv_two)[0]).astype(jnp.bfloat16)
        block_f32 = block_out.astype(jnp.float32)
        previous = jnp.concatenate([jnp.zeros((1,) + block_f32.shape[1:], block_f32.dtype), block_f32[:-1]], axis=0)
        even_frames = jnp.einsum('fhwc,cd->fhwd', block_f32, maps[0], precision=lax.Precision.HIGHEST)
        even_frames = even_frames + jnp.einsum('fhwc,cd->fhwd', previous, maps[1], precision=lax.Precision.HIGHEST)
        odd_frames = jnp.einsum('fhwc,cd->fhwd', block_f32, maps[2], precision=lax.Precision.HIGHEST)
        joined = jnp.stack([even_frames, odd_frames], axis=1)
        return joined.reshape((2 * block_f32.shape[0],) + block_f32.shape[1:]).astype(jnp.bfloat16)
    return lax.map(decode_video, latents)
```

```python
import functools

import jax
import jax.numpy as jnp
from jax import lax
from jax.experimental import pallas as pl
from jax.experimental.pallas import tpu as pltpu
from jax.sharding import PartitionSpec as P

AXES = ("tm", "space")


def moved(value, target):
    count, tiles = lax.axis_size("tm"), lax.axis_size("space")
    pairs = []
    for t in range(count):
        for s in range(tiles):
            to = target(t, s)
            if to is not None and 0 <= to[0] < count:
                pairs.append((t * tiles + s, to[0] * tiles + to[1]))
    return lax.ppermute(value, AXES, pairs)


def swapped(value):
    return moved(value, lambda t, s: (t, s ^ 1))


def to_inner(value, by):
    return moved(value, lambda t, s: (t + by, s ^ 1) if s in (0, 3) else None)


def across(value, by):
    return moved(value, lambda t, s: (t + by, s ^ 2) if s in (0, 3) else None)


def to_outer(value):
    return moved(value, lambda t, s: (t, s ^ 1) if s in (1, 2) else None)


def normed_silu(values, gain):
    mean_square = jnp.mean(values * values, axis=-1, keepdims=True)
    scaled = values * lax.rsqrt(mean_square + 1e-06) * gain
    return scaled * jax.nn.sigmoid(scaled)


def put_shifted(buffer, frame, row, activation):
    rows, width, channels = activation.shape
    zero = jnp.zeros((rows, 1, channels), jnp.float32)
    left = jnp.concatenate([zero, activation[:, :-1]], axis=1)
    right = jnp.concatenate([activation[:, 1:], zero], axis=1)
    for i, part in enumerate((left, activation, right)):
        buffer[frame, pl.ds(row, rows), :, i * channels : (i + 1) * channels] = part.astype(jnp.bfloat16)


def conv(buffer, weight, total, frames, rows):
    channels = total.shape[-1]
    width = buffer.shape[2]

    def tap(i, carry):
        dt, di = i // 3, lax.rem(i, 3)
        lhs = buffer[pl.ds(dt, frames), pl.ds(di, rows)].reshape(frames * rows * width, 3 * channels)
        rhs = weight[i]
        part = jnp.dot(lhs, rhs, preferred_element_type=jnp.float32)

        @pl.when(i == 0)
        def _():
            total[...] = part

        @pl.when(i > 0)
        def _():
            total[...] += part

        return carry

    lax.fori_loop(0, 9, tap, 0)


def block_kernel(
    spot, x, m, p1, p2, p3, q1, q2, q3, z0, z1, z2, z3, gain_one, conv_one, gain_two, conv_two, upsample, out, first, total_one, second, total_two
):
    tile, width, channels = x.shape[1], x.shape[2], x.shape[3]
    s = spot[0]
    even = lax.rem(s, 2) == 0
    inner = jnp.logical_or(s == 1, s == 2)
    own_at = jnp.where(inner, tile, 0)
    mate_at = jnp.where(inner, 0, tile) + jnp.where(even, 0, 2)
    mate_to = jnp.where(even, 6, 0)
    other_to = jnp.where(even, 0, 6)
    gain = gain_one[...].reshape(1, 1, channels)

    def put(frame, row, ref, at, src, rows):
        values = ref[src, pl.ds(at, rows)].astype(jnp.float32)
        put_shifted(first, frame, row, normed_silu(values, gain))

    for f in range(2):
        put(5 + f, 2, x, 0, f, tile)
        put(5 + f, mate_to, m, jnp.where(even, 0, 2), f, 2)

    @pl.when(inner)
    def _():
        for frame, ref, src in ((4, p1, 1), (3, p1, 0), (2, p2, 1), (1, p2, 0), (0, p3, 0)):
            put(frame, 2, ref, own_at, src, tile)
            put(frame, mate_to, ref, mate_at, src, 2)
        for frame, ref, src in ((6, z0, 1), (5, z0, 0), (4, z1, 1), (3, z1, 0), (2, z2, 1), (1, z2, 0), (0, z3, 0)):
            put(frame, other_to, ref, 0, src, 2)

    @pl.when(jnp.logical_not(inner))
    def _():
        for frame, ref, src in ((4, q1, 1), (3, q1, 0), (2, q2, 1), (1, q2, 0), (0, q3, 0)):
            put(frame, 2, ref, own_at, src, tile)
            put(frame, mate_to, ref, mate_at, src, 2)
        for frame in range(7):
            first[frame, pl.ds(other_to, 2)] = jnp.zeros((2, width, 3 * channels), jnp.bfloat16)

    conv(first, conv_one, total_one, 5, 6)
    gain_later = gain_two[...].reshape(1, 1, channels)

    def renorm(f, carry):
        at = pl.multiple_of(f * 6 * width, 6 * width)
        hidden = total_one[pl.ds(at, 6 * width)].reshape(6, width, channels)
        hidden = hidden.astype(jnp.bfloat16).astype(jnp.float32)
        put_shifted(second, f, 0, normed_silu(hidden, gain_later))
        return carry

    lax.fori_loop(0, 5, renorm, 0)

    @pl.when(jnp.logical_not(inner))
    def _():
        edge = jnp.where(even, 0, 5)
        for f in range(5):
            second[f, pl.ds(edge, 1)] = jnp.zeros((1, width, 3 * channels), jnp.bfloat16)

    conv(second, conv_two, total_two, 3, 4)
    cells = tile * width
    before = jnp.where(inner, p1[1, pl.ds(own_at, tile)], q1[1, pl.ds(own_at, tile)])
    block = []
    for f, latents in enumerate((before, x[0], x[1])):
        total = total_two[f * cells : (f + 1) * cells] + latents.reshape(cells, channels).astype(jnp.float32)
        block.append(total.astype(jnp.bfloat16))
    now = jnp.concatenate(block[1:], axis=0)
    earlier = jnp.concatenate(block[:-1], axis=0)
    even_frames = jnp.dot(now, upsample[0], preferred_element_type=jnp.float32)
    even_frames = even_frames + jnp.dot(earlier, upsample[1], preferred_element_type=jnp.float32)
    odd_frames = jnp.dot(now, upsample[2], preferred_element_type=jnp.float32)
    for f in range(2):
        part = slice(f * cells, (f + 1) * cells)
        out[2 * f] = even_frames[part].astype(jnp.bfloat16).reshape(tile, width, channels)
        out[2 * f + 1] = odd_frames[part].astype(jnp.bfloat16).reshape(tile, width, channels)


def local(latents, gain_one, conv_one, gain_two, conv_two, upsample):
    x = latents[0]
    frames, tile, width, channels = x.shape
    s = lax.axis_index("space")
    m = swapped(x)
    chip = jnp.concatenate([x, m], axis=1)
    edge = jnp.where(s < 2, m[:, tile - 2 :], m[:, :2])
    z0 = across(edge, 0)
    p1 = to_inner(chip, 1)
    p2 = to_inner(chip, 2)
    p3 = to_inner(chip[1:], 3)
    z3 = across(edge[1:], 3)
    z2 = across(edge, 2)
    z1 = across(edge, 1)
    q1, q2, q3 = to_outer(p1), to_outer(p2), to_outer(p3)
    vmem = pl.BlockSpec(memory_space=pltpu.VMEM)
    out = pl.pallas_call(
        block_kernel,
        out_shape=jax.ShapeDtypeStruct((2 * frames, tile, width, channels), jnp.bfloat16),
        in_specs=[pl.BlockSpec(memory_space=pltpu.SMEM)] + [vmem] * 17,
        out_specs=vmem,
        scratch_shapes=[
            pltpu.VMEM((7, 8, width, 3 * channels), jnp.bfloat16),
            pltpu.VMEM((5 * 6 * width, channels), jnp.float32),
            pltpu.VMEM((5, 6, width, 3 * channels), jnp.bfloat16),
            pltpu.VMEM((3 * 4 * width, channels), jnp.float32),
        ],
        compiler_params=pltpu.CompilerParams(vmem_limit_bytes=48 * 1024 * 1024),
        name="block",
    )(
        s.reshape(1).astype(jnp.int32), x, m, p1, p2, p3, q1, q2, q3, z0, z1, z2, z3,
        gain_one.reshape(1, channels), conv_one.reshape(9, 3 * channels, channels),
        gain_two.reshape(1, channels), conv_two.reshape(9, 3 * channels, channels), upsample,
    )
    return out[None]


def solution(mesh):
    return jax.shard_map(
        local,
        mesh=mesh,
        in_specs=(P(None, "tm", "space", None, None), P(), P(), P(), P(), P()),
        out_specs=P(None, "tm", "space", None, None),
        check_vma=False,
    )
```
